768 devices in a mesh: dp: 64 (over y, z_lo, core), resp: 12 (over x, z_hi).
Axes of the slice: x: 4, y: 8, z: 12 (z_hi: 3, z_lo: 4; z = z_hi * 4 + z_lo), core: 2. Of those that a mesh axis runs over, the one named last changes fastest.
Arguments:
- queries: bfloat16 [768, 128, 2560], P(('dp', 'resp')), may hold values from -6 to 6
- resp_keys: bfloat16 [768, 128, 512], P(('dp', 'resp')), may hold values from -6 to 6
- resp_values: bfloat16 [768, 128, 512], P(('dp', 'resp')), may hold values from -6 to 6
- grad_out: bfloat16 [768, 128, 2560], P(('dp', 'resp')), may hold values from -6 to 6
- forward_out: bfloat16 [768, 128, 2560], P(('dp', 'resp')), may hold values from -2 to 2
- log_norm: float32 [768, 128, 20], P(('dp', 'resp')), may hold values from 5 to 8
- prompt_keys: bfloat16 [12, 1024, 512], P('resp', 'dp'), may hold values from -6 to 6
- prompt_values: bfloat16 [12, 1024, 512], P('resp', 'dp'), may hold values from -6 to 6
- resp_len: int32 [768], P(('dp', 'resp')), may hold values from 1 to 128, as said below
- seen_blocks: int32 [768], P(('dp', 'resp')), may hold values from 1 to 48, as said below
Outputs:
- grad_queries: bfloat16 [768, 128, 2560], P(('dp', 'resp'))
- grad_resp_keys: bfloat16 [768, 128, 512], P(('dp', 'resp'))
- grad_resp_values: bfloat16 [768, 128, 512], P(('dp', 'resp'))
- grad_prompt_keys: float32 [12, 1024, 512], P('resp', 'dp')
- grad_prompt_values: float32 [12, 1024, 512], P('resp', 'dp')
The draws below stay inside these ranges and needn't reach their ends.
Inputs may be any that keep to these rules, and one draw needn't show every extreme that they name: `resp_len`: some response has all 128 tokens live. `seen_blocks`: some response reads all 48 blocks.
All inputs are finite; a program needn't handle non-finite values.
Results may differ from the reference program's by a relative error of at most 0.009.
Values may be sent and summed in bfloat16 or wider, within the bound.
A program may use at most 32 MiB of HBM per device.

```python
import jax
import jax.numpy as jnp
from jax import lax

HQ = 20
HK = 4
DH = 128
GROUP = 4
RT = 128
PB = 16
RESPONSES = 768
BLOCKS = 48
PROMPT_LEN = 768
PROMPT_ROWS = 1024
N_DP = 64
N_RESP = 12


def draw_resp_len(key, part):
    lens = jax.random.randint(key, (RESPONSES,), 1, RT + 1)
    spot = jax.random.randint(jax.random.fold_in(key, 7), (), 0, RESPONSES)
    return lens.at[spot].set(RT).astype(jnp.int32)


def draw_seen_blocks(key, part):
    base = jax.random.fold_in(key, 11)
    counts = jax.random.randint(base, (RESPONSES,), 1, BLOCKS + 1)
    spot = jax.random.randint(jax.random.fold_in(base, 3), (), 0, RESPONSES)
    return counts.at[spot].set(BLOCKS).astype(jnp.int32)


def steps_of(own_key, shape, cuts, least, high):
    def one(axis_at, parts):
        draws = jax.random.uniform(jax.random.fold_in(jax.random.fold_in(own_key, 6), axis_at), (parts,), jnp.float32, least / len(cuts), high / len(cuts))
        return jnp.repeat(jnp.exp(draws), shape[axis_at] // parts).reshape((-1,) + (1,) * (len(shape) - axis_at - 1))

    loudness = one(*cuts[0])
    for cut in cuts[1:]:
        loudness = loudness * one(*cut)
    return loudness


def scatter_about(rng, extent, spread, limit, pieces=(), kind=jnp.bfloat16):
    values = spread * jax.random.normal(rng, extent, jnp.float32)
    if pieces:
        values = values * steps_of(rng, extent, pieces, -0.22, 0.18)
    return jnp.clip(values, -limit, limit).astype(kind)


def setup_inputs(seed: int = 0) -> dict:
    key_of = jax.random.split(jax.random.key(seed), 11)
    queries = scatter_about(key_of[0], (RESPONSES, RT, HQ * DH), 1.0, 6.0, ((0, 768),))
    resp_keys = scatter_about(key_of[1], (RESPONSES, RT, HK * DH), 1.0, 6.0, ((0, 768),))
    resp_values = scatter_about(key_of[2], (RESPONSES, RT, HK * DH), 1.0, 6.0, ((0, 768),))
    grad_out = scatter_about(key_of[3], (RESPONSES, RT, HQ * DH), 1.0, 6.0, ((0, 768),))
    forward_out = scatter_about(key_of[4], (RESPONSES, RT, HQ * DH), 0.3, 2.0, ((0, 768),))
    log_norm = jnp.clip(5.0 + 3.0 * jax.random.uniform(key_of[5], (RESPONSES, RT, HQ), jnp.float32) ** steps_of(key_of[5], (RESPONSES, RT, HQ), ((0, 768),), -0.2, 0.2), 5.0, 8.0)
    prompt_keys = scatter_about(key_of[6], (N_RESP, PROMPT_ROWS, HK * DH), 1.0, 6.0, ((0, 12), (1, 64)))
    prompt_values = scatter_about(key_of[7], (N_RESP, PROMPT_ROWS, HK * DH), 1.0, 6.0, ((0, 12), (1, 64)))
    resp_len = draw_resp_len(jax.random.fold_in(key_of[10], 71), 0)
    seen_blocks = draw_seen_blocks(jax.random.fold_in(key_of[10], 71), 0)
    return dict(queries=queries, resp_keys=resp_keys, resp_values=resp_values, grad_out=grad_out, forward_out=forward_out, log_norm=log_norm, prompt_keys=prompt_keys, prompt_values=prompt_values, resp_len=resp_len, seen_blocks=seen_blocks)


def pair_grads(q4, do4, lse, delta, keys, vals, visible, scale):
    qf = q4.astype(jnp.float32)
    dof = do4.astype(jnp.float32)
    kf = keys.astype(jnp.float32)
    vf = vals.astype(jnp.float32)
    scores = jnp.einsum('tgrd,kgd->tgrk', qf, kf) * scale
    probs = jnp.where(visible[:, None, None, :], jnp.exp(scores - lse[..., None]), 0.0)
    dprob = jnp.einsum('tgrd,kgd->tgrk', dof, vf)
    dscore = probs * (dprob - delta[..., None])
    probs16 = probs.astype(jnp.bfloat16).astype(jnp.float32)
    dscore16 = dscore.astype(jnp.bfloat16).astype(jnp.float32)
    grad_v = jnp.einsum('tgrk,tgrd->kgd', probs16, dof)
    grad_k = jnp.einsum('tgrk,tgrd->kgd', dscore16, qf) * scale
    grad_q = jnp.einsum('tgrk,kgd->tgrd', dscore16, kf) * scale
    return grad_q, grad_k, grad_v


def reference(queries, resp_keys, resp_values, grad_out, forward_out, log_norm, prompt_keys, prompt_values, resp_len, seen_blocks):
    prompts = N_DP // GROUP
    per = GROUP * N_RESP
    ratio = HQ // HK
    width = HK * DH
    plen = PROMPT_LEN
    scale = 1.0 / (DH ** 0.5)
    pkeys = prompt_keys.reshape(N_RESP, prompts, GROUP * PB, width).transpose(1, 0, 2, 3).reshape(prompts, plen, width)
    pvals = prompt_values.reshape(N_RESP, prompts, GROUP * PB, width).transpose(1, 0, 2, 3).reshape(prompts, plen, width)

    def group_shape(a):
        return a.reshape((prompts, per) + a.shape[1:])

    xs = (pkeys, pvals, group_shape(queries), group_shape(resp_keys), group_shape(resp_values), group_shape(grad_out), group_shape(forward_out), group_shape(log_norm), group_shape(resp_len), group_shape(seen_blocks))

    def one_prompt(args):
        pk, pv, qs, krs, vrs, dos, outs, lses, lens, seens = args

        def one_response(carry, item):
            q, kr, vr, dout, fout, lse, length, seen = item
            q4 = q.reshape(RT, HK, ratio, DH)
            do4 = dout.reshape(RT, HK, ratio, DH)
            o4 = fout.reshape(RT, HK, ratio, DH)
            delta = jnp.sum(do4.astype(jnp.float32) * o4.astype(jnp.float32), axis=-1)
            keys = jnp.concatenate([pk, kr], axis=0).reshape(plen + RT, HK, DH)
            vals = jnp.concatenate([pv, vr], axis=0).reshape(plen + RT, HK, DH)
            place = jnp.arange(plen + RT, dtype=jnp.int32)
            tpos = jnp.arange(RT, dtype=jnp.int32)
            prompt_ok = (place < plen) & (place // PB < seen)
            self_ok = (place[None, :] >= plen) & (place[None, :] - plen <= tpos[:, None])
            visible = (tpos < length)[:, None] & (prompt_ok[None, :] | self_ok)
            gq, gk, gv = pair_grads(q4, do4, lse.reshape(RT, HK, ratio), delta, keys, vals, visible, scale)
            gk = gk.reshape(plen + RT, width)
            gv = gv.reshape(plen + RT, width)
            carry = (carry[0] + gk[:plen], carry[1] + gv[:plen])
            return carry, (gq.reshape(RT, HQ * DH).astype(jnp.bfloat16), gk[plen:].astype(jnp.bfloat16), gv[plen:].astype(jnp.bfloat16))

        zero = jnp.zeros((plen, width), jnp.float32)
        sums, outs_r = lax.scan(one_response, (zero, zero), (qs, krs, vrs, dos, outs, lses, lens, seens))
        return sums[0], sums[1], outs_r[0], outs_r[1], outs_r[2]

    gpk, gpv, gq, gkr, gvr = lax.map(one_prompt, xs)

    def back_layout(a):
        return a.reshape(prompts, N_RESP, GROUP * PB, width).transpose(1, 0, 2, 3).reshape(N_RESP, N_DP * PB, width)

    return (gq.reshape(RESPONSES, RT, HQ * DH), gkr.reshape(RESPONSES, RT, width), gvr.reshape(RESPONSES, RT, width), back_layout(gpk), back_layout(gpv))
```

```python
import jax
import jax.numpy as jnp
from jax import lax
from jax.experimental import pallas as pl
from jax.experimental.pallas import tpu as pltpu
from jax.sharding import PartitionSpec as P

HQ = 20
HK = 4
DH = 128
R = HQ // HK
RT = 128
PB = 16
W = HK * DH
NX = 4
NZ = 6
CT = NZ * 2 * PB
SCALE = 1.0 / DH**0.5
LOG2E = 1.4426950408889634
f32, bf16 = jnp.float32, jnp.bfloat16
NT = (((1,), (1,)), ((), ()))
NN = (((1,), (0,)), ((), ()))
MESH = pl.DeviceIdType.MESH

Z0, ZD, ZR, XP, XM, XR, CG = 0, 1, 3, 5, 11, 17, 23
RC, RA, RB, RZ0, RZ1, RD = 27, 31, 33, 37, 38, 39
NSEM = 41


def dot(a, b, dims):
    return lax.dot_general(a, b, dims, preferred_element_type=f32)


def kernel(
    meta, q_hbm, kr_hbm, vr_hbm, do_hbm, fo_hbm, lse_hbm, pk_hbm, pv_hbm,
    gq_hbm, gkr_hbm, gvr_hbm, gpk_hbm, gpv_hbm,
    q_v, do_v, fo_v, lse_v, kr_v, vr_v, gq_v, gkr_v, gvr_v, gp_v,
    qs, dos, col, rows, gacc,
    buf, part, rc, summed, ra, rb, zsend, rz, rd, agg, own,
    lsem, osem, send, recv,
):
    dp, rs = lax.axis_index("dp"), lax.axis_index("resp")
    base = dp // 4 * 4
    zl, c = dp % 4 // 2, dp % 2
    x, zh = rs // 3, rs % 3
    dn = 2 * zl - 1
    up_zh, down_zh = (zh + 1) % 3, (zh + 2) % 3
    near_zh, far_zh = (zh + dn + 3) % 3, (zh - dn + 3) % 3
    z = zh * 2 + zl
    length, seen = meta[0], meta[1]

    def dev(xx, hh, ll, cc):
        return (base + ll * 2 + cc, xx * 3 + hh)

    right, left = (x + 1) % 4, (x + 3) % 4
    sibling = dev(x, zh, zl, 1 - c)
    partner = dev(x, zh, 1 - zl, c)
    xr, xl = dev(right, zh, zl, c), dev(left, zh, zl, c)
    up, down = dev(x, up_zh, 0, c), dev(x, down_zh, 1, c)
    near = [dev(x, near_zh, i, c) for i in range(2)]

    loads = [
        pltpu.make_async_copy(pk_hbm, buf.at[x, z, c, :, 0:W], lsem.at[0]),
        pltpu.make_async_copy(pv_hbm, buf.at[x, z, c, :, W : 2 * W], lsem.at[1]),
        pltpu.make_async_copy(do_hbm, do_v, lsem.at[2]),
        pltpu.make_async_copy(fo_hbm, fo_v, lsem.at[3]),
        pltpu.make_async_copy(lse_hbm, lse_v, lsem.at[4]),
        pltpu.make_async_copy(q_hbm, q_v, lsem.at[5]),
        pltpu.make_async_copy(kr_hbm, kr_v, lsem.at[6]),
        pltpu.make_async_copy(vr_hbm, vr_v, lsem.at[7]),
    ]
    for copy in loads:
        copy.start()

    barrier = pltpu.get_barrier_semaphore()
    for other in (sibling, partner, xr, xl, near[0], near[1], up, down):
        pl.semaphore_signal(barrier, inc=1, device_id=other, device_id_type=MESH)

    sends = []

    def push(src, dst, index, device):
        copy = pltpu.make_async_remote_copy(
            src_ref=src, dst_ref=dst, send_sem=send.at[len(sends)], recv_sem=recv.at[index],
            device_id=device, device_id_type=MESH,
        )
        copy.start()
        sends.append(copy)

    def arrived(ref, index):
        pltpu.make_async_copy(ref, ref, recv.at[index]).wait()

    for copy in loads[2:5]:
        copy.wait()
    live = lax.broadcasted_iota(jnp.int32, (RT, 1), 0) < length
    col[0, :, 0:HQ] = jnp.where(live, lse_v[...] * LOG2E, 1e30)
    for h in range(HQ):
        sl = slice(h * DH, (h + 1) * DH)
        col[1, :, h : h + 1] = jnp.sum(
            do_v[:, sl].astype(f32) * fo_v[:, sl].astype(f32), axis=1, keepdims=True
        )
    rows[0] = col[0].T
    rows[1] = col[1].T
    loads[5].wait()
    for g in range(HK):
        for r in range(R):
            sl = slice((g * R + r) * DH, (g * R + r + 1) * DH)
            qs[g, r * RT : (r + 1) * RT, :] = q_v[:, sl]
            dos[g, r * RT : (r + 1) * RT, :] = do_v[:, sl]

    loads[0].wait()
    loads[1].wait()
    pl.semaphore_wait(barrier, 8)

    slot_z = [z, zh * 2 + 1 - zl, near_zh * 2, near_zh * 2 + 1, far_zh * 2, far_zh * 2 + 1]

    def block(xx, s):
        return buf.at[xx, slot_z[s], c]

    def spread(s):
        push(block(x, s), block(x, s), XP + s, xr)
        push(block(x, s), block(x, s), XM + s, xl)

    push(block(x, 0), block(x, 0), ZD + zl, up)
    push(block(x, 0), block(x, 0), ZD + zl, down)
    push(block(x, 0), block(x, 0), Z0, partner)
    spread(0)

    def pair(k, v, g, mask):
        qh, dh = qs[g], dos[g]
        lse = jnp.concatenate([rows[0, g * R + r : g * R + r + 1, :] for r in range(R)], axis=1)
        dlt = jnp.concatenate([rows[1, g * R + r : g * R + r + 1, :] for r in range(R)], axis=1)
        p = jnp.exp2(dot(k, qh, NT) * (SCALE * LOG2E) - lse)
        if mask is not None:
            p = jnp.where(mask, p, 0.0)
        ds = (p * (dot(v, dh, NT) - dlt)).astype(bf16)
        gv = dot(p.astype(bf16), dh, NN)
        gk = dot(ds, qh, NN) * SCALE
        return dot(k.T, ds, NN), gk, gv

    loads[6].wait()
    loads[7].wait()
    token = lax.broadcasted_iota(jnp.int32, (RT, R * RT), 0)
    query = lax.broadcasted_iota(jnp.int32, (RT, R * RT), 1) % RT
    for g in range(HK):
        ls = slice(g * DH, (g + 1) * DH)
        gq, gk, gv = pair(kr_v[:, ls], vr_v[:, ls], g, token <= query)
        gkr_v[:, ls] = gk.astype(bf16)
        gvr_v[:, ls] = gv.astype(bf16)
        gacc[g] = gq
    outs = [
        pltpu.make_async_copy(gkr_v, gkr_hbm, osem.at[0]),
        pltpu.make_async_copy(gvr_v, gvr_hbm, osem.at[1]),
    ]
    for copy in outs:
        copy.start()

    arrived(block(x, 1), Z0)
    spread(1)
    for i in range(2):
        arrived(block(x, 2 + i), ZD + i)
        push(block(x, 2 + i), block(x, 2 + i), ZR + i, partner)
        spread(2 + i)
    for i in range(2):
        arrived(block(x, 4 + i), ZR + i)
        spread(4 + i)
    push(buf.at[x, :, c], buf.at[x, :, c], CG, sibling)

    for s in range(NZ):
        arrived(block(left, s), XP + s)
        if s % 2 == 0:
            push(block(left, s), block(left, s), XR + s, xr)
        arrived(block(right, s), XM + s)
        if s % 2 == 1:
            push(block(right, s), block(right, s), XR + s, xl)
    push(buf.at[right, :, c], buf.at[right, :, c], CG + 1, sibling)
    push(buf.at[left, :, c], buf.at[left, :, c], CG + 3, sibling)

    def work(d):
        xx = (x + d) % 4
        arrived(buf.at[xx, :, 1 - c], CG + [0, 1, 2, 3][d])
        seen_here = lax.broadcasted_iota(jnp.int32, (CT, 1), 0) + xx * CT < seen * PB
        none = jnp.zeros((), bf16)
        for g in range(HK):
            ks = slice(g * DH, (g + 1) * DH)
            vs = slice(W + g * DH, W + (g + 1) * DH)
            k = jnp.where(seen_here, buf[xx, :, :, :, ks].reshape(CT, DH), none)
            v = jnp.where(seen_here, buf[xx, :, :, :, vs].reshape(CT, DH), none)
            gq, gk, gv = pair(k, v, g, None)
            gacc[g] += gq
            gk = jnp.where(seen_here, gk, 0.0).astype(bf16)
            gv = jnp.where(seen_here, gv, 0.0).astype(bf16)
            part[xx, :, :, :, ks] = gk.reshape(NZ, 2, PB, DH)
            part[xx, :, :, :, vs] = gv.reshape(NZ, 2, PB, DH)
        push(part.at[xx, :, 1 - c], rc.at[d], RC + d, sibling)

    def core_sum(d, lo, hi):
        xx = (x + d) % 4
        total = part[xx, lo:hi, c].astype(f32) + rc[d, lo:hi].astype(f32)
        return total

    work(0)
    for s in range(NZ):
        arrived(block((x + 2) % 4, s), XR + s)
    push(buf.at[(x + 2) % 4, :, c], buf.at[(x + 2) % 4, :, c], CG + 2, sibling)
    work(1)
    work(2)
    arrived(rc.at[2], RC + 2)
    summed[2] = core_sum(2, 0, NZ).astype(bf16)
    push(summed.at[2, 0:3], ra.at[0], RA, xr)
    push(summed.at[2, 3:6], ra.at[1], RA + 1, xl)
    arrived(rc.at[1], RC + 1)
    summed[1, 3:6] = core_sum(1, 3, 6).astype(bf16)
    push(summed.at[1, 3:6], rb.at[0, 3:6], RB + 1, xr)
    work(3)
    for g in range(HK):
        for r in range(R):
            sl = slice((g * R + r) * DH, (g * R + r + 1) * DH)
            gq_v[:, sl] = (gacc[g, :, r * RT : (r + 1) * RT].T * SCALE).astype(bf16)
    outs.append(pltpu.make_async_copy(gq_v, gq_hbm, osem.at[2]))
    outs[-1].start()
    arrived(rc.at[3], RC + 3)
    summed[3, 0:3] = core_sum(3, 0, 3).astype(bf16)
    push(summed.at[3, 0:3], rb.at[1, 0:3], RB + 2, xl)
    arrived(ra.at[0], RA)
    summed[1, 0:3] = (core_sum(1, 0, 3) + ra[0].astype(f32)).astype(bf16)
    push(summed.at[1, 0:3], rb.at[0, 0:3], RB, xr)
    arrived(ra.at[1], RA + 1)
    summed[3, 3:6] = (core_sum(3, 3, 6) + ra[1].astype(f32)).astype(bf16)
    push(summed.at[3, 3:6], rb.at[1, 3:6], RB + 3, xl)

    arrived(rc.at[0], RC)
    arrived(rb.at[0, 3:6], RB + 1)
    arrived(rb.at[1, 0:3], RB + 2)
    arrived(rb.at[0, 0:3], RB)
    arrived(rb.at[1, 3:6], RB + 3)

    def x_sum(first, count):
        at = pl.ds(first, count)
        return (
            part[x, at, c].astype(f32) + rc[0, at].astype(f32)
        ) + (rb[0, at].astype(f32) + rb[1, at].astype(f32))

    zsend[0:2] = x_sum(far_zh * 2, 2).astype(bf16)
    push(zsend.at[0:2], rz.at[0:2], RZ0, partner)
    zsend[2:3] = x_sum(zh * 2 + 1 - zl, 1).astype(bf16)
    push(zsend.at[2], rz.at[2], RZ1, partner)
    own[...] = x_sum(z, 1)[0]
    agg_own = x_sum(near_zh * 2, 2)
    arrived(rz.at[0:2], RZ0)
    agg[...] = (agg_own + rz[0:2].astype(f32)).astype(bf16)
    for i in range(2):
        push(agg.at[i], rd.at[zl], RD + zl, near[i])
    arrived(rz.at[2], RZ1)
    arrived(rd.at[0], RD)
    arrived(rd.at[1], RD + 1)
    total = (own[...] + rz[2].astype(f32)) + (rd[0].astype(f32) + rd[1].astype(f32))
    gp_v[...] = total
    outs.append(pltpu.make_async_copy(gp_v.at[:, 0:W], gpk_hbm, osem.at[3]))
    outs.append(pltpu.make_async_copy(gp_v.at[:, W : 2 * W], gpv_hbm, osem.at[4]))
    outs[-2].start()
    outs[-1].start()
    for copy in sends:
        copy.wait_send()
    for copy in outs:
        copy.wait()


NSEND = 41


def shards(queries, resp_keys, resp_values, grad_out, forward_out, log_norm, prompt_keys, prompt_values, resp_len, seen_blocks):
    meta = jnp.concatenate([resp_len, seen_blocks])
    shape = jax.ShapeDtypeStruct
    any_space = pl.BlockSpec(memory_space=pl.ANY)
    vmem = pltpu.VMEM
    gq, gkr, gvr, gpk, gpv = pl.pallas_call(
        kernel,
        in_specs=[pl.BlockSpec(memory_space=pltpu.SMEM)] + [any_space] * 8,
        out_specs=[any_space] * 5,
        out_shape=[
            shape((RT, HQ * DH), bf16),
            shape((RT, W), bf16),
            shape((RT, W), bf16),
            shape((PB, W), f32),
            shape((PB, W), f32),
        ],
        scratch_shapes=[
            vmem((RT, HQ * DH), bf16),
            vmem((RT, HQ * DH), bf16),
            vmem((RT, HQ * DH), bf16),
            vmem((RT, HQ), f32),
            vmem((RT, W), bf16),
            vmem((RT, W), bf16),
            vmem((RT, HQ * DH), bf16),
            vmem((RT, W), bf16),
            vmem((RT, W), bf16),
            vmem((PB, 2 * W), f32),
            vmem((HK, R * RT, DH), bf16),
            vmem((HK, R * RT, DH), bf16),
            vmem((2, RT, DH), f32),
            vmem((2, DH, RT), f32),
            vmem((HK, DH, R * RT), f32),
            vmem((NX, NZ, 2, PB, 2 * W), bf16),
            vmem((NX, NZ, 2, PB, 2 * W), bf16),
            vmem((NX, NZ, PB, 2 * W), bf16),
            vmem((NX, NZ, PB, 2 * W), bf16),
            vmem((2, 3, PB, 2 * W), bf16),
            vmem((2, NZ, PB, 2 * W), bf16),
            vmem((3, PB, 2 * W), bf16),
            vmem((3, PB, 2 * W), bf16),
            vmem((2, PB, 2 * W), bf16),
            vmem((2, PB, 2 * W), bf16),
            vmem((PB, 2 * W), f32),
            pltpu.SemaphoreType.DMA((8,)),
            pltpu.SemaphoreType.DMA((5,)),
            pltpu.SemaphoreType.DMA((NSEND,)),
            pltpu.SemaphoreType.DMA((NSEM,)),
        ],
        compiler_params=pltpu.CompilerParams(collective_id=0, has_side_effects=True),
        name="attention_backward",
    )(meta, queries[0], resp_keys[0], resp_values[0], grad_out[0], forward_out[0], log_norm[0], prompt_keys[0], prompt_values[0])
    return gq[None], gkr[None], gvr[None], gpk[None], gpv[None]


def solution(mesh):
    rows = P(("dp", "resp"), None, None)
    prompt = P("resp", "dp", None)
    one = P(("dp", "resp"))
    return jax.shard_map(
        shards,
        mesh=mesh,
        in_specs=(rows,) * 6 + (prompt,) * 2 + (one,) * 2,
        out_specs=(rows,) * 3 + (prompt,) * 2,
        check_vma=False,
    )
```

```python
import jax
import jax.numpy as jnp
from jax import lax
from jax.experimental import pallas as pl
from jax.experimental.pallas import tpu as pltpu
from jax.sharding import PartitionSpec as P

HQ = 20
HK = 4
DH = 128
R = HQ // HK
RT = 128
PB = 16
W = HK * DH
NX = 4
NZ = 6
CT = NZ * 2 * PB
SCALE = 1.0 / DH**0.5
LOG2E = 1.4426950408889634
f32, bf16 = jnp.float32, jnp.bfloat16
NT = (((1,), (1,)), ((), ()))
NN = (((1,), (0,)), ((), ()))
MESH = pl.DeviceIdType.MESH

Z0, ZD, ZR, XP, XM, XR, CG = 0, 1, 3, 5, 11, 17, 23
RC, RA, RB, RZ0, RZ1, RD = 27, 35, 39, 47, 49, 51
NSEM = 55


def dot(a, b, dims):
    return lax.dot_general(a, b, dims, preferred_element_type=f32)


def kernel(
    len_hbm, seen_hbm, q_hbm, kr_hbm, vr_hbm, do_hbm, fo_hbm, lse_hbm, pk_hbm, pv_hbm,
    gq_hbm, gkr_hbm, gvr_hbm, gpk_hbm, gpv_hbm,
    q_v, do_v, fo_v, lse_v, kr_v, vr_v, gq_v, gkr_v, gvr_v, gp_v,
    meta, qs, dos, col, rows, gacc,
    buf, part, rc, summed, ra, rb, zsend, rz, rd, agg, own_near,
    lsem, osem, send, recv,
):
    dp, rs = lax.axis_index("dp"), lax.axis_index("resp")
    base = dp // 4 * 4
    zl, c = dp % 4 // 2, dp % 2
    x, zh = rs // 3, rs % 3
    dn = 2 * zl - 1
    up_zh, down_zh = (zh + 1) % 3, (zh + 2) % 3
    near_zh, far_zh = (zh + dn + 3) % 3, (zh - dn + 3) % 3
    z = zh * 2 + zl

    def dev(xx, hh, ll, cc):
        return (base + ll * 2 + cc, xx * 3 + hh)

    right, left, over = (x + 1) % 4, (x + 3) % 4, (x + 2) % 4
    sibling = dev(x, zh, zl, 1 - c)
    partner = dev(x, zh, 1 - zl, c)
    xr, xl = dev(right, zh, zl, c), dev(left, zh, zl, c)
    up, down = dev(x, up_zh, 0, c), dev(x, down_zh, 1, c)
    near = [dev(x, near_zh, i, c) for i in range(2)]

    loads = [
        pltpu.make_async_copy(pk_hbm, buf.at[x, z, c, :, 0:W], lsem.at[0]),
        pltpu.make_async_copy(pv_hbm, buf.at[x, z, c, :, W : 2 * W], lsem.at[1]),
        pltpu.make_async_copy(do_hbm, do_v, lsem.at[2]),
        pltpu.make_async_copy(fo_hbm, fo_v, lsem.at[3]),
        pltpu.make_async_copy(lse_hbm, lse_v, lsem.at[4]),
        pltpu.make_async_copy(q_hbm, q_v, lsem.at[5]),
        pltpu.make_async_copy(kr_hbm, kr_v, lsem.at[6]),
        pltpu.make_async_copy(vr_hbm, vr_v, lsem.at[7]),
        pltpu.make_async_copy(len_hbm, meta.at[0], lsem.at[8]),
        pltpu.make_async_copy(seen_hbm, meta.at[1], lsem.at[9]),
    ]
    for copy in loads[:2]:
        copy.start()

    barrier = pltpu.get_barrier_semaphore()
    for other in (sibling, partner, xr, xl, near[0], near[1], up, down):
        pl.semaphore_signal(barrier, inc=1, device_id=other, device_id_type=MESH)
    for copy in loads[2:]:
        copy.start()

    sends = []

    def push(src, dst, index, device):
        copy = pltpu.make_async_remote_copy(
            src_ref=src, dst_ref=dst, send_sem=send.at[len(sends)], recv_sem=recv.at[index],
            device_id=device, device_id_type=MESH,
        )
        copy.start()
        sends.append(copy)

    def arrived(ref, index):
        pltpu.make_async_copy(ref, ref, recv.at[index]).wait()

    loads[0].wait()
    loads[1].wait()
    pl.semaphore_wait(barrier, 8)

    slot_z = [z, zh * 2 + 1 - zl, near_zh * 2, near_zh * 2 + 1, far_zh * 2, far_zh * 2 + 1]

    def block(xx, s):
        return buf.at[xx, slot_z[s], c]

    def twin(dx, xx, s):
        push(block(xx, s), block(xx, s), CG + dx, sibling)

    def spread(s):
        push(block(x, s), block(x, s), XP + s, xr)
        push(block(x, s), block(x, s), XM + s, xl)
        twin(0, x, s)

    push(block(x, 0), block(x, 0), ZD + zl, up)
    push(block(x, 0), block(x, 0), ZD + zl, down)
    push(block(x, 0), block(x, 0), Z0, partner)
    spread(0)

    for copy in loads[2:5] + loads[8:]:
        copy.wait()
    length, seen = meta[0, 0], meta[1, 0]
    live = lax.broadcasted_iota(jnp.int32, (1, RT), 1) < length
    for h in range(HQ):
        sl = slice(h * DH, (h + 1) * DH)
        rows[0, h : h + 1, :] = jnp.where(live, lse_v[h] * LOG2E, 1e30)
        col[:, h : h + 1] = jnp.sum(
            do_v[:, sl].astype(f32) * fo_v[:, sl].astype(f32), axis=1, keepdims=True
        )
    rows[1] = col[...].T
    loads[5].wait()
    for g in range(HK):
        for r in range(R):
            sl = slice((g * R + r) * DH, (g * R + r + 1) * DH)
            qs[g, r * RT : (r + 1) * RT, :] = q_v[:, sl]
            dos[g, r * RT : (r + 1) * RT, :] = do_v[:, sl]

    def pair(k, v, g, mask):
        qh, dh = qs[g], dos[g]
        lse = jnp.concatenate([rows[0, g * R + r : g * R + r + 1, :] for r in range(R)], axis=1)
        dlt = jnp.concatenate([rows[1, g * R + r : g * R + r + 1, :] for r in range(R)], axis=1)
        p = jnp.exp2(dot(k, qh, NT) * (SCALE * LOG2E) - lse)
        if mask is not None:
            p = jnp.where(mask, p, 0.0)
        ds = (p * (dot(v, dh, NT) - dlt)).astype(bf16)
        gv = dot(p.astype(bf16), dh, NN)
        gk = dot(ds, qh, NN) * SCALE
        return dot(k.T, ds, NN), gk, gv

    token = lax.broadcasted_iota(jnp.int32, (RT, R * RT), 0)
    query = lax.broadcasted_iota(jnp.int32, (RT, R * RT), 1) % RT

    def own_tokens(g):
        ls = slice(g * DH, (g + 1) * DH)
        gq, gk, gv = pair(kr_v[:, ls], vr_v[:, ls], g, token <= query)
        gkr_v[:, ls] = gk.astype(bf16)
        gvr_v[:, ls] = gv.astype(bf16)
        gacc[g] = gq

    def hand_on(s):
        arrived(block(left, s), XP + s)
        if s % 2 == 0:
            push(block(left, s), block(left, s), XR + s, xr)
        arrived(block(right, s), XM + s)
        if s % 2 == 1:
            push(block(right, s), block(right, s), XR + s, xl)
        twin(3, left, s)
        twin(1, right, s)

    def last_of(s):
        arrived(block(over, s), XR + s)
        twin(2, over, s)

    def work(d, half):
        xx = (x + d) % 4
        if half == 0:
            arrived(buf.at[xx, :, 1 - c], CG + d)
        seen_here = lax.broadcasted_iota(jnp.int32, (CT, 1), 0) + xx * CT < seen * PB
        none = jnp.zeros((), bf16)
        for g in (2 * half, 2 * half + 1):
            ks = slice(g * DH, (g + 1) * DH)
            vs = slice(W + g * DH, W + (g + 1) * DH)
            k = jnp.where(seen_here, buf[xx, :, :, :, ks].reshape(CT, DH), none)
            v = jnp.where(seen_here, buf[xx, :, :, :, vs].reshape(CT, DH), none)
            gq, gk, gv = pair(k, v, g, None)
            gacc[g] += gq
            gk = jnp.where(seen_here, gk, 0.0).astype(bf16)
            gv = jnp.where(seen_here, gv, 0.0).astype(bf16)
            at = 2 * g * DH
            part[xx, :, :, :, at : at + DH] = gk.reshape(NZ, 2, PB, DH)
            part[xx, :, :, :, at + DH : at + 2 * DH] = gv.reshape(NZ, 2, PB, DH)
            head = slice(at, at + 2 * DH)
            push(part.at[xx, :, 1 - c, :, head], rc.at[d, :, :, head], RC + 2 * d + half, sibling)

    halves = [slice(0, W), slice(W, 2 * W)]

    def core_sum(d, lo, hi, h):
        cs = halves[h]
        return part[(x + d) % 4, lo:hi, c, :, cs].astype(f32) + rc[d, lo:hi, :, cs].astype(f32)

    def x_first(d, h):
        cs = halves[h]
        arrived(rc.at[d, :, :, cs], RC + 2 * d + h)
        if d == 2:
            summed[2, :, :, cs] = core_sum(2, 0, NZ, h).astype(bf16)
            push(summed.at[2, 0:3, :, cs], ra.at[0, :, :, cs], RA + 2 * h, xr)
            push(summed.at[2, 3:6, :, cs], ra.at[1, :, :, cs], RA + 2 * h + 1, xl)
        elif d == 1:
            summed[1, 3:6, :, cs] = core_sum(1, 3, 6, h).astype(bf16)
            push(summed.at[1, 3:6, :, cs], rb.at[0, 3:6, :, cs], RB + 4 * h + 1, xr)
        else:
            summed[3, 0:3, :, cs] = core_sum(3, 0, 3, h).astype(bf16)
            push(summed.at[3, 0:3, :, cs], rb.at[1, 0:3, :, cs], RB + 4 * h + 2, xl)

    def x_second(h):
        cs = halves[h]
        arrived(ra.at[0, :, :, cs], RA + 2 * h)
        summed[1, 0:3, :, cs] = (core_sum(1, 0, 3, h) + ra[0, :, :, cs].astype(f32)).astype(bf16)
        push(summed.at[1, 0:3, :, cs], rb.at[0, 0:3, :, cs], RB + 4 * h, xr)
        arrived(ra.at[1, :, :, cs], RA + 2 * h + 1)
        summed[3, 3:6, :, cs] = (core_sum(3, 3, 6, h) + ra[1, :, :, cs].astype(f32)).astype(bf16)
        push(summed.at[3, 3:6, :, cs], rb.at[1, 3:6, :, cs], RB + 4 * h + 3, xl)

    def z_first(h):
        cs = halves[h]
        arrived(rc.at[0, :, :, cs], RC + h)
        arrived(rb.at[0, 3:6, :, cs], RB + 4 * h + 1)
        arrived(rb.at[1, 0:3, :, cs], RB + 4 * h + 2)
        arrived(rb.at[0, 0:3, :, cs], RB + 4 * h)
        arrived(rb.at[1, 3:6, :, cs], RB + 4 * h + 3)

        def x_sum(first, count):
            at = pl.ds(first, count)
            return (
                part[x, at, c, :, cs].astype(f32) + rc[0, at, :, cs].astype(f32)
            ) + (rb[0, at, :, cs].astype(f32) + rb[1, at, :, cs].astype(f32))

        zsend[0:2, :, cs] = x_sum(far_zh * 2, 2).astype(bf16)
        push(zsend.at[0:2, :, cs], rz.at[0:2, :, cs], RZ0 + h, partner)
        own_near[:, :, cs] = x_sum(near_zh * 2, 2)
        zsend[2:3, :, cs] = x_sum(zh * 2 + 1 - zl, 1).astype(bf16)
        push(zsend.at[2, :, cs], rz.at[2, :, cs], RZ1 + h, partner)
        gp_v[:, cs] = x_sum(z, 1)[0]

    def z_second(h):
        cs = halves[h]
        arrived(rz.at[0:2, :, cs], RZ0 + h)
        agg[:, :, cs] = (own_near[:, :, cs] + rz[0:2, :, cs].astype(f32)).astype(bf16)
        for i in range(2):
            push(agg.at[i, :, cs], rd.at[zl, :, cs], RD + 2 * h + zl, near[i])

    def z_third(h):
        cs = halves[h]
        arrived(rz.at[2, :, cs], RZ1 + h)
        arrived(rd.at[0, :, cs], RD + 2 * h)
        arrived(rd.at[1, :, cs], RD + 2 * h + 1)
        gp_v[:, cs] = (gp_v[:, cs] + rz[2, :, cs].astype(f32)) + (
            rd[0, :, cs].astype(f32) + rd[1, :, cs].astype(f32)
        )
        for g in (2 * h, 2 * h + 1):
            sl, at = slice(g * DH, (g + 1) * DH), 2 * g * DH
            outs.append(pltpu.make_async_copy(gp_v.at[:, at : at + DH], gpk_hbm.at[:, sl], osem.at[3 + 2 * g]))
            outs.append(pltpu.make_async_copy(gp_v.at[:, at + DH : at + 2 * DH], gpv_hbm.at[:, sl], osem.at[4 + 2 * g]))
        for copy in outs[-4:]:
            copy.start()

    def from_z(s):
        if s == 1:
            arrived(block(x, 1), Z0)
        elif s < 4:
            arrived(block(x, s), ZD + s - 2)
            push(block(x, s), block(x, s), ZR + s - 2, partner)
        else:
            arrived(block(x, s), ZR + s - 4)
        spread(s)

    loads[6].wait()
    loads[7].wait()
    own_tokens(0)
    own_tokens(1)
    from_z(1)
    own_tokens(2)
    own_tokens(3)
    outs = [
        pltpu.make_async_copy(gkr_v, gkr_hbm, osem.at[0]),
        pltpu.make_async_copy(gvr_v, gvr_hbm, osem.at[1]),
    ]
    for copy in outs:
        copy.start()
    from_z(2)
    from_z(3)
    hand_on(0)
    hand_on(1)
    from_z(4)
    from_z(5)
    hand_on(2)
    hand_on(3)
    last_of(0)
    last_of(1)
    work(0, 0)
    hand_on(4)
    hand_on(5)
    work(0, 1)
    last_of(2)
    last_of(3)
    work(1, 0)
    work(1, 1)
    last_of(4)
    last_of(5)
    work(3, 0)
    x_first(1, 0)
    work(3, 1)
    x_first(1, 1)
    work(2, 0)
    x_first(3, 0)
    work(2, 1)
    x_first(2, 0)
    x_first(3, 1)
    for g in range(HK):
        for r in range(R):
            sl = slice((g * R + r) * DH, (g * R + r + 1) * DH)
            gq_v[:, sl] = (gacc[g, :, r * RT : (r + 1) * RT].T * SCALE).astype(bf16)
    outs.append(pltpu.make_async_copy(gq_v, gq_hbm, osem.at[2]))
    outs[-1].start()
    x_first(2, 1)
    x_second(0)
    x_second(1)
    z_first(0)
    z_first(1)
    z_second(0)
    z_second(1)
    z_third(0)
    z_third(1)
    for copy in sends:
        copy.wait_send()
    for copy in outs:
        copy.wait()


NSEND = 100


def finish(*refs):
    ins, outs, held, sem = refs[:5], refs[5:10], refs[10:15], refs[15]
    pieces = [(1, slice(None)), (2, slice(None)), (3, slice(None)), (4, slice(None))]
    pieces += [(0, slice(i * 32, i * 32 + 32)) for i in range(4)]
    first, last = [], []
    for n, (i, at) in enumerate(pieces):
        first.append(pltpu.make_async_copy(ins[i].at[at], held[i].at[at], sem.at[n]))
        last.append(pltpu.make_async_copy(held[i].at[at], outs[i].at[at], sem.at[8 + n]))
        first[-1].start()
    for n in range(8):
        first[n].wait()
        last[n].start()
    for copy in last:
        copy.wait()


def shards(queries, resp_keys, resp_values, grad_out, forward_out, log_norm, prompt_keys, prompt_values, resp_len, seen_blocks):
    shape = jax.ShapeDtypeStruct
    results = [
        shape((RT, HQ * DH), bf16),
        shape((RT, W), bf16),
        shape((RT, W), bf16),
        shape((PB, W), f32),
        shape((PB, W), f32),
    ]
    any_space = pl.BlockSpec(memory_space=pl.ANY)
    vmem = pltpu.VMEM
    gq, gkr, gvr, gpk, gpv = pl.pallas_call(
        kernel,
        in_specs=[pl.BlockSpec(memory_space=pltpu.HBM)] * 2 + [any_space] * 8,
        out_specs=[any_space] * 5,
        out_shape=results,
        scratch_shapes=[
            vmem((RT, HQ * DH), bf16),
            vmem((RT, HQ * DH), bf16),
            vmem((RT, HQ * DH), bf16),
            vmem((HQ, 1, RT), f32),
            vmem((RT, W), bf16),
            vmem((RT, W), bf16),
            vmem((RT, HQ * DH), bf16),
            vmem((RT, W), bf16),
            vmem((RT, W), bf16),
            vmem((PB, 2 * W), f32),
            pltpu.SMEM((2, 1), jnp.int32),
            vmem((HK, R * RT, DH), bf16),
            vmem((HK, R * RT, DH), bf16),
            vmem((RT, DH), f32),
            vmem((2, DH, RT), f32),
            vmem((HK, DH, R * RT), f32),
            vmem((NX, NZ, 2, PB, 2 * W), bf16),
            vmem((NX, NZ, 2, PB, 2 * W), bf16),
            vmem((NX, NZ, PB, 2 * W), bf16),
            vmem((NX, NZ, PB, 2 * W), bf16),
            vmem((2, 3, PB, 2 * W), bf16),
            vmem((2, NZ, PB, 2 * W), bf16),
            vmem((3, PB, 2 * W), bf16),
            vmem((3, PB, 2 * W), bf16),
            vmem((2, PB, 2 * W), bf16),
            vmem((2, PB, 2 * W), bf16),
            vmem((2, PB, 2 * W), f32),
            pltpu.SemaphoreType.DMA((10,)),
            pltpu.SemaphoreType.DMA((11,)),
            pltpu.SemaphoreType.DMA((NSEND,)),
            pltpu.SemaphoreType.DMA((NSEM,)),
        ],
        compiler_params=pltpu.CompilerParams(collective_id=0, has_side_effects=True),
        name="attention_backward",
    )(
        resp_len, seen_blocks, queries[0], resp_keys[0], resp_values[0], grad_out[0], forward_out[0],
        log_norm.transpose(2, 0, 1), prompt_keys[0], prompt_values[0],
    )
    gq, gkr, gvr, gpk, gpv = pl.pallas_call(
        finish,
        in_specs=[any_space] * 5,
        out_specs=[any_space] * 5,
        out_shape=results,
        scratch_shapes=[vmem(r.shape, r.dtype) for r in results] + [pltpu.SemaphoreType.DMA((16,))],
        name="finish",
    )(gq, gkr, gvr, gpk, gpv)
    return gq[None], gkr[None], gvr[None], gpk[None], gpv[None]


def solution(mesh):
    rows = P(("dp", "resp"), None, None)
    prompt = P("resp", "dp", None)
    one = P(("dp", "resp"))
    return jax.shard_map(
        shards,
        mesh=mesh,
        in_specs=(rows,) * 6 + (prompt,) * 2 + (one,) * 2,
        out_specs=(rows,) * 3 + (prompt,) * 2,
        check_vma=False,
    )
```

```python
import jax
import jax.numpy as jnp
from jax import lax
from jax.experimental import pallas as pl
from jax.experimental.pallas import tpu as pltpu
from jax.sharding import PartitionSpec as P

HQ = 20
HK = 4
DH = 128
R = HQ // HK
RT = 128
PB = 16
W = HK * DH
NX = 4
NZ = 6
CT = NZ * 2 * PB
SCALE = 1.0 / DH**0.5
LOG2E = 1.4426950408889634
f32, bf16 = jnp.float32, jnp.bfloat16
NT = (((1,), (1,)), ((), ()))
NN = (((1,), (0,)), ((), ()))
MESH = pl.DeviceIdType.MESH

Z0, ZD, ZR, XP, XM, XR, CG = 0, 1, 3, 5, 11, 17, 23
RC, RA, RB, RZ0, RZ1, RD = 27, 35, 39, 47, 49, 51
NSEM = 55


def dot(a, b, dims):
    return lax.dot_general(a, b, dims, preferred_element_type=f32)


def kernel(
    len_hbm, seen_hbm, q_hbm, kr_hbm, vr_hbm, do_hbm, fo_hbm, lse_hbm, pk_hbm, pv_hbm,
    gq_v, gkr_v, gvr_v, gpk_v, gpv_v,
    q_v, do_v, fo_v, lse_v, kr_v, vr_v, gp_v,
    meta, qs, dos, col, rows, gacc,
    buf, part, rc, summed, ra, rb, zsend, rz, rd, agg, own_near,
    lsem, send, recv,
):
    dp, rs = lax.axis_index("dp"), lax.axis_index("resp")
    base = dp // 4 * 4
    zl, c = dp % 4 // 2, dp % 2
    x, zh = rs // 3, rs % 3
    dn = 2 * zl - 1
    up_zh, down_zh = (zh + 1) % 3, (zh + 2) % 3
    near_zh, far_zh = (zh + dn + 3) % 3, (zh - dn + 3) % 3
    z = zh * 2 + zl

    def dev(xx, hh, ll, cc):
        return (base + ll * 2 + cc, xx * 3 + hh)

    right, left, over = (x + 1) % 4, (x + 3) % 4, (x + 2) % 4
    sibling = dev(x, zh, zl, 1 - c)
    partner = dev(x, zh, 1 - zl, c)
    xr, xl = dev(right, zh, zl, c), dev(left, zh, zl, c)
    up, down = dev(x, up_zh, 0, c), dev(x, down_zh, 1, c)
    near = [dev(x, near_zh, i, c) for i in range(2)]

    loads = [
        pltpu.make_async_copy(pk_hbm, buf.at[x, z, c, :, 0:W], lsem.at[0]),
        pltpu.make_async_copy(pv_hbm, buf.at[x, z, c, :, W : 2 * W], lsem.at[1]),
        pltpu.make_async_copy(do_hbm, do_v, lsem.at[2]),
        pltpu.make_async_copy(fo_hbm, fo_v, lsem.at[3]),
        pltpu.make_async_copy(lse_hbm, lse_v, lsem.at[4]),
        pltpu.make_async_copy(q_hbm, q_v, lsem.at[5]),
        pltpu.make_async_copy(kr_hbm, kr_v, lsem.at[6]),
        pltpu.make_async_copy(vr_hbm, vr_v, lsem.at[7]),
        pltpu.make_async_copy(len_hbm, meta.at[0], lsem.at[8]),
        pltpu.make_async_copy(seen_hbm, meta.at[1], lsem.at[9]),
    ]
    for copy in loads[:2]:
        copy.start()

    barrier = pltpu.get_barrier_semaphore()
    for other in (sibling, partner, xr, xl, near[0], near[1], up, down):
        pl.semaphore_signal(barrier, inc=1, device_id=other, device_id_type=MESH)
    for copy in loads[2:]:
        copy.start()

    sends = []

    def push(src, dst, index, device):
        copy = pltpu.make_async_remote_copy(
            src_ref=src, dst_ref=dst, send_sem=send.at[len(sends)], recv_sem=recv.at[index],
            device_id=device, device_id_type=MESH,
        )
        copy.start()
        sends.append(copy)

    def arrived(ref, index):
        pltpu.make_async_copy(ref, ref, recv.at[index]).wait()

    loads[0].wait()
    loads[1].wait()
    pl.semaphore_wait(barrier, 8)

    slot_z = [z, zh * 2 + 1 - zl, near_zh * 2, near_zh * 2 + 1, far_zh * 2, far_zh * 2 + 1]

    def block(xx, s):
        return buf.at[xx, slot_z[s], c]

    def twin(dx, xx, s):
        push(block(xx, s), block(xx, s), CG + dx, sibling)

    def spread(s):
        push(block(x, s), block(x, s), XP + s, xr)
        push(block(x, s), block(x, s), XM + s, xl)
        twin(0, x, s)

    push(block(x, 0), block(x, 0), ZD + zl, up)
    push(block(x, 0), block(x, 0), ZD + zl, down)
    push(block(x, 0), block(x, 0), Z0, partner)
    spread(0)

    for copy in loads[2:5] + loads[8:]:
        copy.wait()
    length, seen = meta[0, 0], meta[1, 0]
    live = lax.broadcasted_iota(jnp.int32, (1, RT), 1) < length
    for h in range(HQ):
        sl = slice(h * DH, (h + 1) * DH)
        rows[0, h : h + 1, :] = jnp.where(live, lse_v[h] * LOG2E, 1e30)
        col[:, h : h + 1] = jnp.sum(
            do_v[:, sl].astype(f32) * fo_v[:, sl].astype(f32), axis=1, keepdims=True
        )
    rows[1] = col[...].T
    loads[5].wait()
    for g in range(HK):
        for r in range(R):
            sl = slice((g * R + r) * DH, (g * R + r + 1) * DH)
            qs[g, r * RT : (r + 1) * RT, :] = q_v[:, sl]
            dos[g, r * RT : (r + 1) * RT, :] = do_v[:, sl]

    def pair(k, v, g, mask):
        qh, dh = qs[g], dos[g]
        lse = jnp.concatenate([rows[0, g * R + r : g * R + r + 1, :] for r in range(R)], axis=1)
        dlt = jnp.concatenate([rows[1, g * R + r : g * R + r + 1, :] for r in range(R)], axis=1)
        p = jnp.exp2(dot(k, qh, NT) * (SCALE * LOG2E) - lse)
        if mask is not None:
            p = jnp.where(mask, p, 0.0)
        ds = (p * (dot(v, dh, NT) - dlt)).astype(bf16)
        gv = dot(p.astype(bf16), dh, NN)
        gk = dot(ds, qh, NN) * SCALE
        return dot(k.T, ds, NN), gk, gv

    token = lax.broadcasted_iota(jnp.int32, (RT, R * RT), 0)
    query = lax.broadcasted_iota(jnp.int32, (RT, R * RT), 1) % RT

    def own_tokens(g):
        ls = slice(g * DH, (g + 1) * DH)
        gq, gk, gv = pair(kr_v[:, ls], vr_v[:, ls], g, token <= query)
        gkr_v[:, ls] = gk.astype(bf16)
        gvr_v[:, ls] = gv.astype(bf16)
        gacc[g] = gq

    def hand_on(s):
        arrived(block(left, s), XP + s)
        if s % 2 == 0:
            push(block(left, s), block(left, s), XR + s, xr)
        arrived(block(right, s), XM + s)
        if s % 2 == 1:
            push(block(right, s), block(right, s), XR + s, xl)
        twin(3, left, s)
        twin(1, right, s)

    def last_of(s):
        arrived(block(over, s), XR + s)
        twin(2, over, s)

    def work(d, half):
        xx = (x + d) % 4
        if half == 0:
            arrived(buf.at[xx, :, 1 - c], CG + d)
        seen_here = lax.broadcasted_iota(jnp.int32, (CT, 1), 0) + xx * CT < seen * PB
        none = jnp.zeros((), bf16)
        for g in (2 * half, 2 * half + 1):
            ks = slice(g * DH, (g + 1) * DH)
            vs = slice(W + g * DH, W + (g + 1) * DH)
            k = jnp.where(seen_here, buf[xx, :, :, :, ks].reshape(CT, DH), none)
            v = jnp.where(seen_here, buf[xx, :, :, :, vs].reshape(CT, DH), none)
            gq, gk, gv = pair(k, v, g, None)
            gacc[g] += gq
            gk = jnp.where(seen_here, gk, 0.0).astype(bf16)
            gv = jnp.where(seen_here, gv, 0.0).astype(bf16)
            at = 2 * g * DH
            part[xx, :, :, :, at : at + DH] = gk.reshape(NZ, 2, PB, DH)
            part[xx, :, :, :, at + DH : at + 2 * DH] = gv.reshape(NZ, 2, PB, DH)
            head = slice(at, at + 2 * DH)
            push(part.at[xx, :, 1 - c, :, head], rc.at[d, :, :, head], RC + 2 * d + half, sibling)

    halves = [slice(0, W), slice(W, 2 * W)]

    def core_sum(d, lo, hi, h):
        cs = halves[h]
        return part[(x + d) % 4, lo:hi, c, :, cs].astype(f32) + rc[d, lo:hi, :, cs].astype(f32)

    def x_first(d, h):
        cs = halves[h]
        arrived(rc.at[d, :, :, cs], RC + 2 * d + h)
        if d == 2:
            summed[2, :, :, cs] = core_sum(2, 0, NZ, h).astype(bf16)
            push(summed.at[2, 0:3, :, cs], ra.at[0, :, :, cs], RA + 2 * h, xr)
            push(summed.at[2, 3:6, :, cs], ra.at[1, :, :, cs], RA + 2 * h + 1, xl)
        elif d == 1:
            summed[1, 3:6, :, cs] = core_sum(1, 3, 6, h).astype(bf16)
            push(summed.at[1, 3:6, :, cs], rb.at[0, 3:6, :, cs], RB + 4 * h + 1, xr)
        else:
            summed[3, 0:3, :, cs] = core_sum(3, 0, 3, h).astype(bf16)
            push(summed.at[3, 0:3, :, cs], rb.at[1, 0:3, :, cs], RB + 4 * h + 2, xl)

    def x_second(h):
        cs = halves[h]
        arrived(ra.at[0, :, :, cs], RA + 2 * h)
        summed[1, 0:3, :, cs] = (core_sum(1, 0, 3, h) + ra[0, :, :, cs].astype(f32)).astype(bf16)
        push(summed.at[1, 0:3, :, cs], rb.at[0, 0:3, :, cs], RB + 4 * h, xr)
        arrived(ra.at[1, :, :, cs], RA + 2 * h + 1)
        summed[3, 3:6, :, cs] = (core_sum(3, 3, 6, h) + ra[1, :, :, cs].astype(f32)).astype(bf16)
        push(summed.at[3, 3:6, :, cs], rb.at[1, 3:6, :, cs], RB + 4 * h + 3, xl)

    def z_first(h):
        cs = halves[h]
        arrived(rc.at[0, :, :, cs], RC + h)
        arrived(rb.at[0, 3:6, :, cs], RB + 4 * h + 1)
        arrived(rb.at[1, 0:3, :, cs], RB + 4 * h + 2)
        arrived(rb.at[0, 0:3, :, cs], RB + 4 * h)
        arrived(rb.at[1, 3:6, :, cs], RB + 4 * h + 3)

        def x_sum(first, count):
            at = pl.ds(first, count)
            return (
                part[x, at, c, :, cs].astype(f32) + rc[0, at, :, cs].astype(f32)
            ) + (rb[0, at, :, cs].astype(f32) + rb[1, at, :, cs].astype(f32))

        zsend[0:2, :, cs] = x_sum(far_zh * 2, 2).astype(bf16)
        push(zsend.at[0:2, :, cs], rz.at[0:2, :, cs], RZ0 + h, partner)
        own_near[:, :, cs] = x_sum(near_zh * 2, 2)
        zsend[2:3, :, cs] = x_sum(zh * 2 + 1 - zl, 1).astype(bf16)
        push(zsend.at[2, :, cs], rz.at[2, :, cs], RZ1 + h, partner)
        gp_v[:, cs] = x_sum(z, 1)[0]

    def z_second(h):
        cs = halves[h]
        arrived(rz.at[0:2, :, cs], RZ0 + h)
        agg[:, :, cs] = (own_near[:, :, cs] + rz[0:2, :, cs].astype(f32)).astype(bf16)
        for i in range(2):
            push(agg.at[i, :, cs], rd.at[zl, :, cs], RD + 2 * h + zl, near[i])

    def z_third(h):
        cs = halves[h]
        arrived(rz.at[2, :, cs], RZ1 + h)
        arrived(rd.at[0, :, cs], RD + 2 * h)
        arrived(rd.at[1, :, cs], RD + 2 * h + 1)
        gp_v[:, cs] = (gp_v[:, cs] + rz[2, :, cs].astype(f32)) + (
            rd[0, :, cs].astype(f32) + rd[1, :, cs].astype(f32)
        )
        for g in (2 * h, 2 * h + 1):
            sl, at = slice(g * DH, (g + 1) * DH), 2 * g * DH
            gpk_v[:, sl] = gp_v[:, at : at + DH]
            gpv_v[:, sl] = gp_v[:, at + DH : at + 2 * DH]

    def from_z(s):
        if s == 1:
            arrived(block(x, 1), Z0)
        elif s < 4:
            arrived(block(x, s), ZD + s - 2)
            push(block(x, s), block(x, s), ZR + s - 2, partner)
        else:
            arrived(block(x, s), ZR + s - 4)
        spread(s)

    loads[6].wait()
    loads[7].wait()
    own_tokens(0)
    own_tokens(1)
    from_z(1)
    own_tokens(2)
    own_tokens(3)
    from_z(2)
    from_z(3)
    hand_on(0)
    hand_on(1)
    from_z(4)
    from_z(5)
    hand_on(2)
    hand_on(3)
    last_of(0)
    last_of(1)
    work(0, 0)
    hand_on(4)
    hand_on(5)
    work(1, 0)
    last_of(2)
    last_of(3)
    work(3, 0)
    work(0, 1)
    last_of(4)
    last_of(5)
    x_first(1, 0)
    work(1, 1)
    x_first(3, 0)
    work(2, 0)
    x_first(1, 1)
    work(3, 1)
    x_first(2, 0)
    work(2, 1)
    x_first(3, 1)
    for g in range(HK):
        for r in range(R):
            sl = slice((g * R + r) * DH, (g * R + r + 1) * DH)
            gq_v[:, sl] = (gacc[g, :, r * RT : (r + 1) * RT].T * SCALE).astype(bf16)
    x_first(2, 1)
    x_second(0)
    x_second(1)
    z_first(0)
    z_first(1)
    z_second(0)
    z_second(1)
    z_third(0)
    z_third(1)
    for copy in sends:
        copy.wait_send()


NSEND = 100


def finish(*refs):
    sem = refs[10]
    copies = [pltpu.make_async_copy(refs[i], refs[5 + i], sem.at[i]) for i in range(5)]
    for copy in copies:
        copy.start()
    for copy in copies:
        copy.wait()


def shards(queries, resp_keys, resp_values, grad_out, forward_out, log_norm, prompt_keys, prompt_values, resp_len, seen_blocks):
    shape = jax.ShapeDtypeStruct
    results = [
        shape((RT, HQ * DH), bf16),
        shape((RT, W), bf16),
        shape((RT, W), bf16),
        shape((PB, W), f32),
        shape((PB, W), f32),
    ]
    any_space = pl.BlockSpec(memory_space=pl.ANY)
    vmem = pltpu.VMEM
    gq, gkr, gvr, gpk, gpv = pl.pallas_call(
        kernel,
        in_specs=[pl.BlockSpec(memory_space=pltpu.HBM)] * 2 + [any_space] * 8,
        out_specs=[pl.BlockSpec(memory_space=pltpu.VMEM)] * 5,
        out_shape=[vmem(r.shape, r.dtype) for r in results],
        scratch_shapes=[
            vmem((RT, HQ * DH), bf16),
            vmem((RT, HQ * DH), bf16),
            vmem((RT, HQ * DH), bf16),
            vmem((HQ, 1, RT), f32),
            vmem((RT, W), bf16),
            vmem((RT, W), bf16),
            vmem((PB, 2 * W), f32),
            pltpu.SMEM((2, 1), jnp.int32),
            vmem((HK, R * RT, DH), bf16),
            vmem((HK, R * RT, DH), bf16),
            vmem((RT, DH), f32),
            vmem((2, DH, RT), f32),
            vmem((HK, DH, R * RT), f32),
            vmem((NX, NZ, 2, PB, 2 * W), bf16),
            vmem((NX, NZ, 2, PB, 2 * W), bf16),
            vmem((NX, NZ, PB, 2 * W), bf16),
            vmem((NX, NZ, PB, 2 * W), bf16),
            vmem((2, 3, PB, 2 * W), bf16),
            vmem((2, NZ, PB, 2 * W), bf16),
            vmem((3, PB, 2 * W), bf16),
            vmem((3, PB, 2 * W), bf16),
            vmem((2, PB, 2 * W), bf16),
            vmem((2, PB, 2 * W), bf16),
            vmem((2, PB, 2 * W), f32),
            pltpu.SemaphoreType.DMA((10,)),
            pltpu.SemaphoreType.DMA((NSEND,)),
            pltpu.SemaphoreType.DMA((NSEM,)),
        ],
        compiler_params=pltpu.CompilerParams(collective_id=0, has_side_effects=True),
        name="attention_backward",
    )(
        resp_len, seen_blocks, queries[0], resp_keys[0], resp_values[0], grad_out[0], forward_out[0],
        log_norm.transpose(2, 0, 1), prompt_keys[0], prompt_values[0],
    )
    gq, gkr, gvr, gpk, gpv = pl.pallas_call(
        finish,
        in_specs=[any_space] * 5,
        out_specs=[any_space] * 5,
        out_shape=results,
        scratch_shapes=[pltpu.SemaphoreType.DMA((5,))],
        name="finish",
    )(*(pltpu.with_memory_space_constraint(r, pltpu.VMEM) for r in (gq, gkr, gvr, gpk, gpv)))
    return gq[None], gkr[None], gvr[None], gpk[None], gpv[None]


def solution(mesh):
    rows = P(("dp", "resp"), None, None)
    prompt = P("resp", "dp", None)
    one = P(("dp", "resp"))
    return jax.shard_map(
        shards,
        mesh=mesh,
        in_specs=(rows,) * 6 + (prompt,) * 2 + (one,) * 2,
        out_specs=(rows,) * 3 + (prompt,) * 2,
        check_vma=False,
    )
```

```python
import jax
import jax.numpy as jnp
from jax import lax
from jax.experimental import pallas as pl
from jax.experimental.pallas import tpu as pltpu
from jax.sharding import PartitionSpec as P

HQ = 20
HK = 4
DH = 128
R = HQ // HK
RT = 128
PB = 16
W = HK * DH
NX = 4
NZ = 6
CT = NZ * 2 * PB
SCALE = 1.0 / DH**0.5
LOG2E = 1.4426950408889634
f32, bf16 = jnp.float32, jnp.bfloat16
NT = (((1,), (1,)), ((), ()))
NN = (((1,), (0,)), ((), ()))
MESH = pl.DeviceIdType.MESH

Z0, ZD, ZR, XP, XM, XR, CG = 0, 1, 3, 5, 11, 17, 23
RC, RA, RB, RZ0, RZ1, RD = 27, 35, 39, 47, 49, 51
NSEM = 55


def dot(a, b, dims):
    return lax.dot_general(a, b, dims, preferred_element_type=f32)


def kernel(
    len_hbm, seen_hbm, q_hbm, kr_hbm, vr_hbm, do_hbm, fo_hbm, lse_hbm, pk_hbm, pv_hbm,
    gq_v, gkr_v, gvr_v, gpk_v, gpv_v,
    q_v, do_v, fo_v, lse_v, kr_v, vr_v, gp_v,
    meta, qs, dos, col, rows, gacc,
    buf, part, rc, summed, ra, rb, zsend, rz, rd, agg, own_near,
    lsem, send, recv,
):
    dp, rs = lax.axis_index("dp"), lax.axis_index("resp")
    base = dp // 4 * 4
    zl, c = dp % 4 // 2, dp % 2
    x, zh = rs // 3, rs % 3
    dn = 2 * zl - 1
    up_zh, down_zh = (zh + 1) % 3, (zh + 2) % 3
    near_zh, far_zh = (zh + dn + 3) % 3, (zh - dn + 3) % 3
    z = zh * 2 + zl

    def dev(xx, hh, ll, cc):
        return (base + ll * 2 + cc, xx * 3 + hh)

    right, left, over = (x + 1) % 4, (x + 3) % 4, (x + 2) % 4
    sibling = dev(x, zh, zl, 1 - c)
    partner = dev(x, zh, 1 - zl, c)
    xr, xl = dev(right, zh, zl, c), dev(left, zh, zl, c)
    up, down = dev(x, up_zh, 0, c), dev(x, down_zh, 1, c)
    near = [dev(x, near_zh, i, c) for i in range(2)]

    loads = [
        pltpu.make_async_copy(pk_hbm, buf.at[x, z, c, :, 0:W], lsem.at[0]),
        pltpu.make_async_copy(pv_hbm, buf.at[x, z, c, :, W : 2 * W], lsem.at[1]),
        pltpu.make_async_copy(do_hbm, do_v, lsem.at[2]),
        pltpu.make_async_copy(fo_hbm, fo_v, lsem.at[3]),
        pltpu.make_async_copy(lse_hbm, lse_v, lsem.at[4]),
        pltpu.make_async_copy(q_hbm, q_v, lsem.at[5]),
        pltpu.make_async_copy(kr_hbm, kr_v, lsem.at[6]),
        pltpu.make_async_copy(vr_hbm, vr_v, lsem.at[7]),
        pltpu.make_async_copy(len_hbm, meta.at[0], lsem.at[8]),
        pltpu.make_async_copy(seen_hbm, meta.at[1], lsem.at[9]),
    ]
    for copy in loads[:2]:
        copy.start()

    barrier = pltpu.get_barrier_semaphore()
    for other in (sibling, partner, xr, xl, near[0], near[1], up, down):
        pl.semaphore_signal(barrier, inc=1, device_id=other, device_id_type=MESH)
    for copy in loads[2:]:
        copy.start()

    sends = []

    def push(src, dst, index, device):
        copy = pltpu.make_async_remote_copy(
            src_ref=src, dst_ref=dst, send_sem=send.at[len(sends)], recv_sem=recv.at[index],
            device_id=device, device_id_type=MESH,
        )
        copy.start()
        sends.append(copy)

    def arrived(ref, index):
        pltpu.make_async_copy(ref, ref, recv.at[index]).wait()

    loads[0].wait()
    loads[1].wait()
    pl.semaphore_wait(barrier, 8)

    slot_z = [z, zh * 2 + 1 - zl, near_zh * 2, near_zh * 2 + 1, far_zh * 2, far_zh * 2 + 1]

    def block(xx, s):
        return buf.at[xx, slot_z[s], c]

    def twin(dx, xx, s):
        push(block(xx, s), block(xx, s), CG + dx, sibling)

    def spread(s):
        push(block(x, s), block(x, s), XP + s, xr)
        push(block(x, s), block(x, s), XM + s, xl)
        twin(0, x, s)

    push(block(x, 0), block(x, 0), ZD + zl, up)
    push(block(x, 0), block(x, 0), ZD + zl, down)
    push(block(x, 0), block(x, 0), Z0, partner)
    spread(0)

    for copy in loads[2:5] + loads[8:]:
        copy.wait()
    length, seen = meta[0, 0], meta[1, 0]
    live = lax.broadcasted_iota(jnp.int32, (1, RT), 1) < length
    for h in range(HQ):
        sl = slice(h * DH, (h + 1) * DH)
        rows[0, h : h + 1, :] = jnp.where(live, lse_v[h] * LOG2E, 1e30)
        col[:, h : h + 1] = jnp.sum(
            do_v[:, sl].astype(f32) * fo_v[:, sl].astype(f32), axis=1, keepdims=True
        )
    rows[1] = col[...].T
    loads[5].wait()
    for g in range(HK):
        for r in range(R):
            sl = slice((g * R + r) * DH, (g * R + r + 1) * DH)
            qs[g, r * RT : (r + 1) * RT, :] = q_v[:, sl]
            dos[g, r * RT : (r + 1) * RT, :] = do_v[:, sl]

    def pair(k, v, g, mask):
        qh, dh = qs[g], dos[g]
        lse = jnp.concatenate([rows[0, g * R + r : g * R + r + 1, :] for r in range(R)], axis=1)
        dlt = jnp.concatenate([rows[1, g * R + r : g * R + r + 1, :] for r in range(R)], axis=1)
        p = jnp.exp2(dot(k, qh, NT) * (SCALE * LOG2E) - lse)
        if mask is not None:
            p = jnp.where(mask, p, 0.0)
        ds = (p * (dot(v, dh, NT) - dlt)).astype(bf16)
        gv = dot(p.astype(bf16), dh, NN)
        gk = dot(ds, qh, NN) * SCALE
        return dot(k.T, ds, NN), gk, gv

    token = lax.broadcasted_iota(jnp.int32, (RT, R * RT), 0)
    query = lax.broadcasted_iota(jnp.int32, (RT, R * RT), 1) % RT

    def own_tokens(g):
        ls = slice(g * DH, (g + 1) * DH)
        gq, gk, gv = pair(kr_v[:, ls], vr_v[:, ls], g, token <= query)
        gkr_v[:, ls] = gk.astype(bf16)
        gvr_v[:, ls] = gv.astype(bf16)
        gacc[g] = gq

    def hand_on(s):
        arrived(block(left, s), XP + s)
        if s % 2 == 0:
            push(block(left, s), block(left, s), XR + s, xr)
        arrived(block(right, s), XM + s)
        if s % 2 == 1:
            push(block(right, s), block(right, s), XR + s, xl)
        twin(3, left, s)
        twin(1, right, s)

    def last_of(s):
        arrived(block(over, s), XR + s)
        twin(2, over, s)

    def work(d, half):
        xx = (x + d) % 4
        if half == 0:
            arrived(buf.at[xx, :, 1 - c], CG + d)
        seen_here = lax.broadcasted_iota(jnp.int32, (CT, 1), 0) + xx * CT < seen * PB
        none = jnp.zeros((), bf16)
        for g in (2 * half, 2 * half + 1):
            ks = slice(g * DH, (g + 1) * DH)
            vs = slice(W + g * DH, W + (g + 1) * DH)
            k = jnp.where(seen_here, buf[xx, :, :, :, ks].reshape(CT, DH), none)
            v = jnp.where(seen_here, buf[xx, :, :, :, vs].reshape(CT, DH), none)
            gq, gk, gv = pair(k, v, g, None)
            gacc[g] += gq
            gk = jnp.where(seen_here, gk, 0.0).astype(bf16)
            gv = jnp.where(seen_here, gv, 0.0).astype(bf16)
            at = 2 * g * DH
            part[xx, :, :, :, at : at + DH] = gk.reshape(NZ, 2, PB, DH)
            part[xx, :, :, :, at + DH : at + 2 * DH] = gv.reshape(NZ, 2, PB, DH)
            head = slice(at, at + 2 * DH)
            push(part.at[xx, :, 1 - c, :, head], rc.at[d, :, :, head], RC + 2 * d + half, sibling)

    halves = [slice(0, W), slice(W, 2 * W)]

    def core_sum(d, lo, hi, h):
        cs = halves[h]
        return part[(x + d) % 4, lo:hi, c, :, cs].astype(f32) + rc[d, lo:hi, :, cs].astype(f32)

    def x_first(d, h):
        cs = halves[h]
        arrived(rc.at[d, :, :, cs], RC + 2 * d + h)
        if d == 2:
            summed[2, :, :, cs] = core_sum(2, 0, NZ, h).astype(bf16)
            push(summed.at[2, 0:3, :, cs], ra.at[0, :, :, cs], RA + 2 * h, xr)
            push(summed.at[2, 3:6, :, cs], ra.at[1, :, :, cs], RA + 2 * h + 1, xl)
        elif d == 1:
            summed[1, 3:6, :, cs] = core_sum(1, 3, 6, h).astype(bf16)
            push(summed.at[1, 3:6, :, cs], rb.at[0, 3:6, :, cs], RB + 4 * h + 1, xr)
        else:
            summed[3, 0:3, :, cs] = core_sum(3, 0, 3, h).astype(bf16)
            push(summed.at[3, 0:3, :, cs], rb.at[1, 0:3, :, cs], RB + 4 * h + 2, xl)

    def x_second(h):
        cs = halves[h]
        arrived(ra.at[0, :, :, cs], RA + 2 * h)
        summed[1, 0:3, :, cs] = (core_sum(1, 0, 3, h) + ra[0, :, :, cs].astype(f32)).astype(bf16)
        push(summed.at[1, 0:3, :, cs], rb.at[0, 0:3, :, cs], RB + 4 * h, xr)
        arrived(ra.at[1, :, :, cs], RA + 2 * h + 1)
        summed[3, 3:6, :, cs] = (core_sum(3, 3, 6, h) + ra[1, :, :, cs].astype(f32)).astype(bf16)
        push(summed.at[3, 3:6, :, cs], rb.at[1, 3:6, :, cs], RB + 4 * h + 3, xl)

    def z_first(h):
        cs = halves[h]
        arrived(rc.at[0, :, :, cs], RC + h)
        arrived(rb.at[0, 3:6, :, cs], RB + 4 * h + 1)
        arrived(rb.at[1, 0:3, :, cs], RB + 4 * h + 2)
        arrived(rb.at[0, 0:3, :, cs], RB + 4 * h)
        arrived(rb.at[1, 3:6, :, cs], RB + 4 * h + 3)

        def x_sum(first, count):
            at = pl.ds(first, count)
            return (
                part[x, at, c, :, cs].astype(f32) + rc[0, at, :, cs].astype(f32)
            ) + (rb[0, at, :, cs].astype(f32) + rb[1, at, :, cs].astype(f32))

        zsend[0:2, :, cs] = x_sum(far_zh * 2, 2).astype(bf16)
        push(zsend.at[0:2, :, cs], rz.at[0:2, :, cs], RZ0 + h, partner)
        own_near[:, :, cs] = x_sum(near_zh * 2, 2)
        zsend[2:3, :, cs] = x_sum(zh * 2 + 1 - zl, 1).astype(bf16)
        push(zsend.at[2, :, cs], rz.at[2, :, cs], RZ1 + h, partner)
        gp_v[:, cs] = x_sum(z, 1)[0]

    def z_second(h):
        cs = halves[h]
        arrived(rz.at[0:2, :, cs], RZ0 + h)
        agg[:, :, cs] = (own_near[:, :, cs] + rz[0:2, :, cs].astype(f32)).astype(bf16)
        for i in range(2):
            push(agg.at[i, :, cs], rd.at[zl, :, cs], RD + 2 * h + zl, near[i])

    def z_third(h):
        cs = halves[h]
        arrived(rz.at[2, :, cs], RZ1 + h)
        arrived(rd.at[0, :, cs], RD + 2 * h)
        arrived(rd.at[1, :, cs], RD + 2 * h + 1)
        gp_v[:, cs] = (gp_v[:, cs] + rz[2, :, cs].astype(f32)) + (
            rd[0, :, cs].astype(f32) + rd[1, :, cs].astype(f32)
        )
        for g in (2 * h, 2 * h + 1):
            sl, at = slice(g * DH, (g + 1) * DH), 2 * g * DH
            gpk_v[:, sl] = gp_v[:, at : at + DH]
            gpv_v[:, sl] = gp_v[:, at + DH : at + 2 * DH]

    def from_z(s):
        if s == 1:
            arrived(block(x, 1), Z0)
        elif s < 4:
            arrived(block(x, s), ZD + s - 2)
            push(block(x, s), block(x, s), ZR + s - 2, partner)
        else:
            arrived(block(x, s), ZR + s - 4)
        spread(s)

    loads[6].wait()
    loads[7].wait()
    own_tokens(0)
    own_tokens(1)
    from_z(1)
    from_z(2)
    from_z(3)
    own_tokens(2)
    hand_on(0)
    own_tokens(3)
    hand_on(1)
    from_z(4)
    from_z(5)
    hand_on(2)
    hand_on(3)
    last_of(0)
    last_of(1)
    work(0, 0)
    hand_on(4)
    hand_on(5)
    work(1, 0)
    last_of(2)
    last_of(3)
    work(3, 0)
    work(0, 1)
    last_of(4)
    last_of(5)
    x_first(1, 0)
    work(1, 1)
    x_first(3, 0)
    work(2, 0)
    x_first(1, 1)
    work(3, 1)
    x_first(2, 0)
    work(2, 1)
    for g in range(HK):
        for r in range(R):
            sl = slice((g * R + r) * DH, (g * R + r + 1) * DH)
            gq_v[:, sl] = (gacc[g, :, r * RT : (r + 1) * RT].T * SCALE).astype(bf16)
    x_first(2, 1)
    x_first(3, 1)
    x_second(0)
    x_second(1)
    z_first(0)
    z_first(1)
    z_second(0)
    z_second(1)
    z_third(0)
    z_third(1)
    for copy in sends:
        copy.wait_send()


NSEND = 100


def finish(*refs):
    sem = refs[10]
    copies = [pltpu.make_async_copy(refs[i], refs[5 + i], sem.at[i]) for i in range(5)]
    for copy in copies:
        copy.start()
    for copy in copies:
        copy.wait()


def shards(queries, resp_keys, resp_values, grad_out, forward_out, log_norm, prompt_keys, prompt_values, resp_len, seen_blocks):
    shape = jax.ShapeDtypeStruct
    results = [
        shape((RT, HQ * DH), bf16),
        shape((RT, W), bf16),
        shape((RT, W), bf16),
        shape((PB, W), f32),
        shape((PB, W), f32),
    ]
    any_space = pl.BlockSpec(memory_space=pl.ANY)
    vmem = pltpu.VMEM
    gq, gkr, gvr, gpk, gpv = pl.pallas_call(
        kernel,
        in_specs=[pl.BlockSpec(memory_space=pltpu.HBM)] * 2 + [any_space] * 8,
        out_specs=[pl.BlockSpec(memory_space=pltpu.VMEM)] * 5,
        out_shape=[vmem(r.shape, r.dtype) for r in results],
        scratch_shapes=[
            vmem((RT, HQ * DH), bf16),
            vmem((RT, HQ * DH), bf16),
            vmem((RT, HQ * DH), bf16),
            vmem((HQ, 1, RT), f32),
            vmem((RT, W), bf16),
            vmem((RT, W), bf16),
            vmem((PB, 2 * W), f32),
            pltpu.SMEM((2, 1), jnp.int32),
            vmem((HK, R * RT, DH), bf16),
            vmem((HK, R * RT, DH), bf16),
            vmem((RT, DH), f32),
            vmem((2, DH, RT), f32),
            vmem((HK, DH, R * RT), f32),
            vmem((NX, NZ, 2, PB, 2 * W), bf16),
            vmem((NX, NZ, 2, PB, 2 * W), bf16),
            vmem((NX, NZ, PB, 2 * W), bf16),
            vmem((NX, NZ, PB, 2 * W), bf16),
            vmem((2, 3, PB, 2 * W), bf16),
            vmem((2, NZ, PB, 2 * W), bf16),
            vmem((3, PB, 2 * W), bf16),
            vmem((3, PB, 2 * W), bf16),
            vmem((2, PB, 2 * W), bf16),
            vmem((2, PB, 2 * W), bf16),
            vmem((2, PB, 2 * W), f32),
            pltpu.SemaphoreType.DMA((10,)),
            pltpu.SemaphoreType.DMA((NSEND,)),
            pltpu.SemaphoreType.DMA((NSEM,)),
        ],
        compiler_params=pltpu.CompilerParams(collective_id=0, has_side_effects=True),
        name="attention_backward",
    )(
        resp_len, seen_blocks, queries[0], resp_keys[0], resp_values[0], grad_out[0], forward_out[0],
        log_norm.transpose(2, 0, 1), prompt_keys[0], prompt_values[0],
    )
    gq, gkr, gvr, gpk, gpv = pl.pallas_call(
        finish,
        in_specs=[any_space] * 5,
        out_specs=[any_space] * 5,
        out_shape=results,
        scratch_shapes=[pltpu.SemaphoreType.DMA((5,))],
        name="finish",
    )(*(pltpu.with_memory_space_constraint(r, pltpu.VMEM) for r in (gq, gkr, gvr, gpk, gpv)))
    return gq[None], gkr[None], gvr[None], gpk[None], gpv[None]


def solution(mesh):
    rows = P(("dp", "resp"), None, None)
    prompt = P("resp", "dp", None)
    one = P(("dp", "resp"))
    return jax.shard_map(
        shards,
        mesh=mesh,
        in_specs=(rows,) * 6 + (prompt,) * 2 + (one,) * 2,
        out_specs=(rows,) * 3 + (prompt,) * 2,
        check_vma=False,
    )
```
